32 devices in a mesh: cols: 32 (over z, y, x, core).
Axes of the slice: x: 2, y: 2, z: 4, core: 2. Of those that a mesh axis runs over, the one named last changes fastest.
Arguments:
- gcm_state: float32 [2, 72, 16384], P(None, None, 'cols'), may hold values from -6 to 6
- crm_state: bfloat16 [2, 58, 32, 16384], P(None, None, None, 'cols'), may hold values from -6 to 6
- span_map: int32 [16384], P('cols'), may hold values from 0 to 16383, as said below
- crm_cost: int32 [16384], P('cols'), may hold values from 1 to 58
- neighbours: int32 [4096, 8], P('cols'), may hold values from -1 to 4095, as said below
Outputs:
- crm_next: bfloat16 [2, 58, 32, 16384], P(None, None, None, 'cols')
- smoothed: float32 [2, 72, 16384], P(None, None, 'cols')
The draws below stay inside these ranges and needn't reach their ends.
Inputs may be any that keep to these rules, and one draw needn't show every extreme that they name: `span_map`: A permutation of the span positions; position p is held by device p // 512. The columns of each device go, exactly 32 each, to 16 distinct devices, its own among them, and each device receives exactly 32 columns from each of 16 devices. `neighbours`: -1 marks an empty slot and stands only in the last slot; every other entry names an element of the element's own device or of one of the two devices beside it along cols, wrapping around.
All inputs are finite; a program needn't handle non-finite values.
Results may differ from the reference program's by a relative error of at most 0.001.
Values sent between devices are 32-bit elements; how exact they have to be, the bound alone decides.
A program may use at most 128 MiB of HBM per device.

```python
import jax
import jax.numpy as jnp
from jax import lax

LEV = 72
CRM_NX = 32
CRM_LEV = 58
PCOL = 4
NBR = 8
SUBSTEPS = 2
ELEM_DEV = 128
COL_DEV = 512
NELEM = 4096
NCOL = 16384
CAP = 32
HALF = 16


def draw_span_map(key, part):
    devices = NCOL // COL_DEV
    key_order = jax.random.fold_in(key, 11)
    key_shift = jax.random.fold_in(key, 12)
    key_local = jax.random.fold_in(key, 13)
    key_place = jax.random.fold_in(key, 14)
    ordering = jax.random.permutation(key_order, devices).astype(jnp.int32)
    inverse = jnp.argsort(ordering).astype(jnp.int32)
    drawn_shifts = (jax.random.permutation(key_shift, devices - 1)[:HALF - 1] + 1).astype(jnp.int32)
    shifts = jnp.concatenate([jnp.zeros((1,), jnp.int32), drawn_shifts])
    local_order = jax.vmap(lambda single: jax.random.permutation(single, COL_DEV))(jax.random.split(key_local, devices)).astype(jnp.int32)
    places = jax.vmap(lambda single: jax.random.permutation(single, COL_DEV))(jax.random.split(key_place, devices)).astype(jnp.int32)
    ranking = jnp.arange(COL_DEV, dtype=jnp.int32)
    grouping = ranking // CAP
    source = jnp.arange(devices, dtype=jnp.int32)
    target = inverse[(ordering[:, None] + shifts[grouping][None, :]) % devices]
    position = target * COL_DEV + places[target, ranking[None, :]]
    columns = source[:, None] * COL_DEV + local_order
    return jnp.zeros((NCOL,), jnp.int32).at[columns.reshape(-1)].set(position.reshape(-1).astype(jnp.int32))


def draw_neighbours(key, part):
    key_near = jax.random.fold_in(key, 21)
    key_edge = jax.random.fold_in(key, 22)
    element = jnp.arange(NELEM, dtype=jnp.int32)
    owner = element // ELEM_DEV
    offset = jax.random.randint(key_near, (NELEM, NBR), 0, 3 * ELEM_DEV).astype(jnp.int32)
    chosen = (((owner - 1) * ELEM_DEV)[:, None] + offset) % NELEM
    chosen = chosen.at[0, 0].set(NELEM - 1)
    corner = jax.random.randint(key_edge, (NELEM,), 0, 8) == 0
    corner = corner.at[0].set(True)
    slot_ids = jnp.arange(NBR, dtype=jnp.int32)
    padded = corner[:, None] & (slot_ids[None, :] == NBR - 1)
    return jnp.where(padded, -1, chosen).astype(jnp.int32)


def place_ends(result, key, least, top_value):
    dims = result.shape
    index_at = [jax.random.randint(jax.random.fold_in(key, axis), (), 0, dims[axis]) for axis in range(len(dims))]
    result = result.at[tuple(index_at)].set(least)
    longest = dims.index(max(dims))
    index_at[longest] = (index_at[longest] + 1) % dims[longest]
    return result.at[tuple(index_at)].set(top_value)


def shard_levels(own_key, extent, pieces, least, largest):
    gain, own = 1.0, jax.random.fold_in(own_key, 6)
    for dim, blocks in pieces:
        steps = jnp.exp(jax.random.uniform(jax.random.fold_in(own, dim), (blocks,), jnp.float32, least / len(pieces), largest / len(pieces)))
        gain = gain * jnp.repeat(steps, extent[dim] // blocks).reshape([-1 if axis == dim else 1 for axis in range(len(extent))])
    return gain


def bell_draw(stream_key, shape, width, limit, cuts=(), kind=jnp.bfloat16):
    values = jax.random.normal(stream_key, shape, jnp.float32) * width
    if len(cuts) > 0:
        values = shard_levels(stream_key, shape, cuts, -0.22, 0.18) * values
    return jnp.clip(values, min=-limit, max=limit).astype(kind)


def setup_inputs(seed: int = 0) -> dict:
    key_of = jax.random.split(jax.random.key(seed), 6)
    return {
        "gcm_state": bell_draw(key_of[0], (2, LEV, NCOL), 1.0, 6.0, ((2, 32),), jnp.float32),
        "crm_state": bell_draw(key_of[1], (2, CRM_LEV, CRM_NX, NCOL), 1.0, 6.0, ((3, 32),)),
        "span_map": draw_span_map(jax.random.fold_in(key_of[5], 71), 0),
        "crm_cost": place_ends(jax.random.randint(key_of[3], (NCOL,), 1, CRM_LEV + 1), jax.random.fold_in(key_of[3], 1), 1, CRM_LEV).astype(jnp.int32),
        "neighbours": draw_neighbours(jax.random.fold_in(key_of[5], 71), 0),
    }


RELAX = 0.5
STEP = 0.5
MIXING = 0.2
LATENT = 0.6
SMOOTHING = 0.5


def interpolation(rows_out, rows_in):
    target = jnp.arange(rows_out, dtype=jnp.int32)[:, None]
    source = jnp.arange(rows_in, dtype=jnp.int32)[None, :]
    scaled = target * (rows_in - 1)
    lower = scaled // (rows_out - 1)
    weight = (scaled - lower * (rows_out - 1)).astype(jnp.float32) / (rows_out - 1)
    upper = jnp.minimum(lower + 1, rows_in - 1)
    return jnp.where(source == lower, 1.0 - weight, 0.0) + jnp.where(source == upper, weight, 0.0)


def crm_steps(fields, forcing, active):
    levels = fields.shape[1]
    height = jnp.arange(levels, dtype=jnp.float32)
    saturation = (1.0 - 0.8 * height / (levels - 1))[:, None, None]
    for substep in range(SUBSTEPS):
        sideways = jnp.roll(fields, 1, axis=2) + jnp.roll(fields, -1, axis=2) - 2.0 * fields
        upper_cells = jnp.concatenate([fields[:, 1:], fields[:, -1:]], axis=1)
        lower_cells = jnp.concatenate([fields[:, :1], fields[:, :-1]], axis=1)
        vertical = upper_cells + lower_cells - 2.0 * fields
        fields = fields + STEP * (forcing[:, :, None, :] + MIXING * (sideways + vertical))
        condensed = jnp.maximum(fields[1] - saturation, 0.0) * active[:, None, :]
        fields = jnp.stack([fields[0] + LATENT * condensed, fields[1] - condensed])
    return fields


def physics(crm_old, profile, cloud_top):
    start = crm_old.astype(jnp.float32)
    start_mean = jnp.mean(start, axis=2)
    forcing = RELAX * (profile - start_mean)
    levels = crm_old.shape[1]
    active = (jnp.arange(levels, dtype=jnp.int32)[:, None] < cloud_top[None, :]).astype(jnp.float32)
    final = crm_steps(start, forcing, active)
    change = jnp.mean(final, axis=2) - start_mean
    return final.astype(jnp.bfloat16), change


def run_block(parts):
    return physics(parts[0], parts[1], parts[2])


def reference(gcm_state, crm_state, span_map, crm_cost, neighbours):
    interp_down = interpolation(CRM_LEV, LEV)
    interp_up = interpolation(LEV, CRM_LEV)
    profile = jnp.einsum("jk,fkc->fjc", interp_down, gcm_state, precision=lax.Precision.HIGHEST)
    span_profile = jnp.zeros_like(profile).at[:, :, span_map].set(profile)
    span_top = jnp.zeros((NCOL,), jnp.int32).at[span_map].set(crm_cost)
    devices = NCOL // COL_DEV
    block_state = jnp.moveaxis(crm_state.reshape(2, CRM_LEV, CRM_NX, devices, COL_DEV), 3, 0)
    block_profile = jnp.moveaxis(span_profile.reshape(2, CRM_LEV, devices, COL_DEV), 2, 0)
    block_top = span_top.reshape(devices, COL_DEV)
    finals, changes = lax.map(run_block, (block_state, block_profile, block_top))
    crm_next = jnp.moveaxis(finals, 0, 3).reshape(2, CRM_LEV, CRM_NX, NCOL)
    change = jnp.moveaxis(changes, 0, 2).reshape(2, CRM_LEV, NCOL)
    tendency = jnp.einsum("kj,fjc->fkc", interp_up, change, precision=lax.Precision.HIGHEST)
    updated = gcm_state + tendency[:, :, span_map]
    edge_mean = jnp.mean(updated.reshape(2, LEV, NELEM, PCOL), axis=3)
    valid = neighbours >= 0
    lookup = jnp.where(valid, neighbours, 0)
    gathered = edge_mean[:, :, lookup] * valid.astype(jnp.float32)[None, None]
    neighbour_sum = jnp.sum(gathered, axis=3)
    count = jnp.sum(valid.astype(jnp.float32), axis=1)
    pull = SMOOTHING * (neighbour_sum / count[None, None, :] - edge_mean)
    smoothed = updated + jnp.repeat(pull, PCOL, axis=2)
    return crm_next, smoothed
```

```python
import functools

import numpy as np
import jax
import jax.numpy as jnp
from jax import lax
from jax.experimental import pallas as pl
from jax.experimental.pallas import tpu as pltpu
from jax.sharding import PartitionSpec as P

LEV = 72
CRM_NX = 32
CRM_LEV = 58
PCOL = 4
NBR = 8
FEATURES = 2 * CRM_LEV
WIDTH = 128
CHUNK = 256

RELAX = 0.5
STEP = 0.5
MIXING = 0.2
LATENT = 0.6
SMOOTHING = 0.5

MESH = pl.DeviceIdType.MESH
F32 = jnp.float32
BF16 = jnp.bfloat16


def interpolation(rows_out, rows_in):
    target = np.arange(rows_out, dtype=np.int32)[:, None]
    source = np.arange(rows_in, dtype=np.int32)[None, :]
    scaled = target * (rows_in - 1)
    lower = scaled // (rows_out - 1)
    weight = (scaled - lower * (rows_out - 1)).astype(np.float32) / np.float32(rows_out - 1)
    upper = np.minimum(lower + 1, rows_in - 1)
    zero = np.float32(0.0)
    return np.where(source == lower, np.float32(1.0) - weight, zero) + np.where(
        source == upper, weight, zero
    )


def both_fields(rows_out, rows_in, height, width):
    matrix = np.zeros((height, width), np.float32)
    block = interpolation(rows_out, rows_in)
    matrix[:rows_out, :rows_in] = block
    matrix[rows_out : 2 * rows_out, rows_in : 2 * rows_in] = block
    return matrix


def halves(values):
    high = values.astype(BF16)
    low = (values - high.astype(F32)).astype(BF16)
    return high, low


def dot(a, b, dims):
    return lax.dot_general(a, b, (dims, ((), ())), preferred_element_type=F32)


AB = ((1,), (0,))
ABT = ((1,), (1,))


def split_dot(values, chosen, dims):
    rows = values.shape[0]
    both = dot(jnp.concatenate(halves(values), axis=0), chosen, dims)
    return both[:rows] + both[rows:]


def onehot(mask):
    return jnp.where(mask, 1.0, 0.0).astype(BF16)


def kernel(
    devices,
    gcm_ref,
    crm_ref,
    span_ref,
    cost_ref,
    near_ref,
    down_ref,
    up_ref,
    next_ref,
    smooth_ref,
    crm_buf,
    fields,
    next_buf,
    pick_out,
    pick_in,
    sent,
    arrived,
    sent_back,
    arrived_back,
    start_mean,
    forcing,
    change,
    own_mean,
    near_mean,
    near_pick,
    load_sem,
    store_sem,
    out_send,
    out_recv,
    back_send,
    back_recv,
    near_send,
    near_recv,
):
    me = lax.axis_index("cols")
    columns = gcm_ref.shape[1]
    elements = near_ref.shape[0]
    capacity = sent.shape[1]
    slots = devices * capacity
    column_bits = columns.bit_length() - 1

    barrier = pltpu.get_barrier_semaphore()

    def greet(k, carry):
        pl.semaphore_signal(
            barrier, inc=1, device_id=(lax.rem(me + k, devices),), device_id_type=MESH
        )
        return carry

    lax.fori_loop(1, devices, greet, 0)

    load = pltpu.make_async_copy(crm_ref, crm_buf.at[:, pl.ds(1, CRM_LEV)], load_sem)
    load.start()

    span = span_ref[...]
    target = lax.shift_right_logical(span, column_bits)
    place = jnp.bitwise_and(span, columns - 1)
    peers = lax.broadcasted_iota(jnp.int32, (devices, columns), 0)
    mine = peers == target
    first = lax.broadcasted_iota(jnp.int32, (columns, columns), 0)
    second = lax.broadcasted_iota(jnp.int32, (columns, columns), 1)
    before = dot(onehot(mine), onehot(first < second), AB)
    slot = before + (peers * capacity).astype(F32)
    position = jnp.sum(jnp.where(mine, slot, 0.0), axis=0, keepdims=True).astype(jnp.int32)

    profile = lax.dot_general(
        down_ref[...],
        gcm_ref[...],
        (AB, ((), ())),
        precision=lax.Precision.HIGHEST,
        preferred_element_type=F32,
    )
    row = lax.broadcasted_iota(jnp.int32, (WIDTH, columns), 0)
    message = jnp.where(row == FEATURES, (place + 1).astype(F32), profile)
    message = jnp.where(row == FEATURES + 1, cost_ref[...].astype(F32), message)
    message_parts = jnp.concatenate(halves(message), axis=0)

    peers_chunk = CHUNK // capacity
    for chunk in range(slots // CHUNK):
        index = lax.broadcasted_iota(jnp.int32, (CHUNK, columns), 0) + chunk * CHUNK
        chosen = onehot(index == position)
        pick_out[chunk * CHUNK : (chunk + 1) * CHUNK, :] = chosen
        packed = dot(chosen, message_parts, ABT)
        packed = packed[:, :WIDTH] + packed[:, WIDTH:]
        sent[chunk * peers_chunk : (chunk + 1) * peers_chunk] = packed.reshape(
            peers_chunk, capacity, WIDTH
        )

    pl.semaphore_wait(barrier, devices - 1)

    def relay(source, landing, send_sem, recv_sem):
        def send(k, carry):
            peer = lax.rem(me + k, devices)
            pltpu.make_async_remote_copy(
                src_ref=source.at[peer],
                dst_ref=landing.at[me],
                send_sem=send_sem,
                recv_sem=recv_sem,
                device_id=(peer,),
                device_id_type=MESH,
            ).start()
            return carry

        lax.fori_loop(1, devices, send, 0)
        landing[me] = source[me]
        return pltpu.make_async_remote_copy(
            src_ref=source.at[pl.ds(0, devices - 1)],
            dst_ref=landing.at[pl.ds(0, devices - 1)],
            send_sem=send_sem,
            recv_sem=recv_sem,
            device_id=(lax.rem(me + 1, devices),),
            device_id_type=MESH,
        )

    outward = relay(sent, arrived, out_send, out_recv)

    load.wait()
    for field in range(2):
        crm_buf[field, 0] = crm_buf[field, 1]
        crm_buf[field, CRM_LEV + 1] = crm_buf[field, CRM_LEV]

    def stencil(here, above, below):
        sideways = pltpu.roll(here, 1, 0) + pltpu.roll(here, CRM_NX - 1, 0)
        return here + (STEP * MIXING) * ((sideways + (above + below)) - 4.0 * here)

    def prepare(j, carry):
        for field in range(2):
            here = crm_buf[field, j + 1].astype(F32)
            above = crm_buf[field, j + 2].astype(F32)
            below = crm_buf[field, j].astype(F32)
            fields[field, j + 1] = stencil(here, above, below)
            start_mean[pl.ds(field * CRM_LEV + j, 1), :] = jnp.sum(
                here, axis=0, keepdims=True
            ) * (1.0 / CRM_NX)
        return carry

    lax.fori_loop(0, CRM_LEV, prepare, 0)

    near = near_ref[...]
    total = devices * elements
    offset = near - (me - 1) * elements
    offset = jnp.where(offset < 0, offset + total, offset)
    offset = jnp.where(offset >= total, offset - total, offset)
    offset = jnp.where(near >= 0, offset, -1)
    spots = lax.broadcasted_iota(jnp.int32, (elements, 3 * elements), 1)
    chosen = jnp.zeros((elements, 3 * elements), F32)
    for s in range(NBR):
        chosen = chosen + jnp.where(offset[:, s : s + 1] == spots, 1.0, 0.0)
    near_pick[...] = chosen.astype(BF16)

    outward.wait_recv()
    landed = arrived[...].reshape(slots, WIDTH)
    labels = landed[:, FEATURES : FEATURES + 1].astype(jnp.int32)
    columns_at = lax.broadcasted_iota(jnp.int32, (slots, columns), 1) + 1
    pick_in[...] = onehot(labels == columns_at)
    placed = split_dot(landed.T, pick_in[...], AB)
    top = placed[FEATURES + 1 : FEATURES + 2, :]
    forcing[...] = (STEP * RELAX) * (placed[:FEATURES] - start_mean[...])

    def condense(j, heat, moisture):
        level = j.astype(F32)
        saturation = 1.0 - 0.8 * level / (CRM_LEV - 1)
        active = jnp.where(level < top, 1.0, 0.0)
        condensed = jnp.maximum(moisture - saturation, 0.0) * active
        return heat + LATENT * condensed, moisture - condensed

    def push(j):
        return forcing[pl.ds(j, 1), :], forcing[pl.ds(CRM_LEV + j, 1), :]

    def first_step(j, carry):
        push0, push1 = push(j)
        heat, moisture = condense(j, fields[0, j + 1] + push0, fields[1, j + 1] + push1)
        fields[0, j + 1] = heat
        fields[1, j + 1] = moisture
        return carry

    lax.fori_loop(0, CRM_LEV, first_step, 0)
    for field in range(2):
        fields[field, 0] = fields[field, 1]
        fields[field, CRM_LEV + 1] = fields[field, CRM_LEV]

    change[FEATURES:, :] = jnp.zeros((WIDTH - FEATURES, columns), F32)

    def second_step(j, carry):
        push0, push1 = push(j)
        heat = stencil(fields[0, j + 1], fields[0, j + 2], fields[0, j]) + push0
        moisture = stencil(fields[1, j + 1], fields[1, j + 2], fields[1, j]) + push1
        heat, moisture = condense(j, heat, moisture)
        for field, final in ((0, heat), (1, moisture)):
            next_buf[field, j] = final.astype(BF16)
            at = pl.ds(field * CRM_LEV + j, 1)
            change[at, :] = (
                jnp.sum(final, axis=0, keepdims=True) * (1.0 / CRM_NX) - start_mean[at, :]
            )
        return carry

    lax.fori_loop(0, CRM_LEV, second_step, 0)

    change_parts = jnp.concatenate(halves(change[...]), axis=0)
    for chunk in range(slots // CHUNK):
        packed = dot(pick_in[chunk * CHUNK : (chunk + 1) * CHUNK, :], change_parts, ABT)
        packed = packed[:, :WIDTH] + packed[:, WIDTH:]
        sent_back[chunk * peers_chunk : (chunk + 1) * peers_chunk] = packed.reshape(
            peers_chunk, capacity, WIDTH
        )
    inward = relay(sent_back, arrived_back, back_send, back_recv)
    store = pltpu.make_async_copy(next_buf, next_ref, store_sem)
    store.start()

    inward.wait_recv()
    own = split_dot(arrived_back[...].reshape(slots, WIDTH).T, pick_out[...], AB)
    tendency = lax.dot_general(
        up_ref[...],
        own,
        (AB, ((), ())),
        precision=lax.Precision.HIGHEST,
        preferred_element_type=F32,
    )
    updated = gcm_ref[...] + tendency
    member = lax.broadcasted_iota(jnp.int32, (elements, columns), 1)
    lowest = lax.broadcasted_iota(jnp.int32, (elements, columns), 0) * PCOL
    inside = onehot((member >= lowest) & (member < lowest + PCOL))
    own_mean[...] = split_dot(updated, inside, ABT) * (1.0 / PCOL)

    exchanges = []
    for side in range(2):
        peer = lax.rem(me + 1, devices) if side == 0 else lax.rem(me + devices - 1, devices)
        exchange = pltpu.make_async_remote_copy(
            src_ref=own_mean,
            dst_ref=near_mean.at[side],
            send_sem=near_send.at[side],
            recv_sem=near_recv.at[side],
            device_id=(peer,),
            device_id_type=MESH,
        )
        exchange.start()
        exchanges.append(exchange)
    edge_mean = own_mean[...]
    ones = jnp.ones((8, 3 * elements), BF16)
    count = dot(ones, near_pick[...], ABT)[:1]
    scale = 1.0 / count
    total_near = split_dot(edge_mean, near_pick[:, elements : 2 * elements], ABT)
    for side in range(2):
        exchanges[side].wait_recv()
        spot = 2 * side * elements
        total_near = total_near + split_dot(
            near_mean[side], near_pick[:, spot : spot + elements], ABT
        )
    pull = SMOOTHING * (total_near * scale - edge_mean)
    smooth_ref[...] = updated + split_dot(pull, inside, AB)

    outward.wait_send()
    inward.wait_send()
    for exchange in exchanges:
        exchange.wait_send()
    store.wait()


def on_device(devices, gcm_state, crm_state, span_map, crm_cost, neighbours):
    columns = gcm_state.shape[2]
    elements = neighbours.shape[0]
    capacity = 2 * columns // devices
    slots = devices * capacity
    down = jnp.asarray(both_fields(CRM_LEV, LEV, WIDTH, 2 * LEV))
    up = jnp.asarray(both_fields(LEV, CRM_LEV, 2 * LEV, WIDTH))
    vmem = pl.BlockSpec(memory_space=pltpu.VMEM)
    anywhere = pl.BlockSpec(memory_space=pl.ANY)
    relay = pltpu.VMEM((devices, capacity, WIDTH), F32)
    crm_next, smoothed = pl.pallas_call(
        functools.partial(kernel, devices),
        out_shape=(
            jax.ShapeDtypeStruct(crm_state.shape, BF16),
            jax.ShapeDtypeStruct((2 * LEV, columns), F32),
        ),
        in_specs=[vmem, anywhere, vmem, vmem, vmem, vmem, vmem],
        out_specs=(anywhere, vmem),
        scratch_shapes=[
            pltpu.VMEM((2, CRM_LEV + 2, CRM_NX, columns), BF16),
            pltpu.VMEM((2, CRM_LEV + 2, CRM_NX, columns), F32),
            pltpu.VMEM((2, CRM_LEV, CRM_NX, columns), BF16),
            pltpu.VMEM((slots, columns), BF16),
            pltpu.VMEM((slots, columns), BF16),
            relay,
            relay,
            relay,
            relay,
            pltpu.VMEM((FEATURES, columns), F32),
            pltpu.VMEM((FEATURES, columns), F32),
            pltpu.VMEM((WIDTH, columns), F32),
            pltpu.VMEM((2 * LEV, elements), F32),
            pltpu.VMEM((2, 2 * LEV, elements), F32),
            pltpu.VMEM((elements, 3 * elements), BF16),
            pltpu.SemaphoreType.DMA,
            pltpu.SemaphoreType.DMA,
            pltpu.SemaphoreType.DMA,
            pltpu.SemaphoreType.DMA,
            pltpu.SemaphoreType.DMA,
            pltpu.SemaphoreType.DMA,
            pltpu.SemaphoreType.DMA((2,)),
            pltpu.SemaphoreType.DMA((2,)),
        ],
        compiler_params=pltpu.CompilerParams(
            collective_id=0, has_side_effects=True, vmem_limit_bytes=60 * 1024 * 1024
        ),
    )(
        gcm_state.reshape(2 * LEV, columns),
        crm_state,
        span_map.reshape(1, columns),
        crm_cost.reshape(1, columns),
        neighbours,
        down,
        up,
    )
    return crm_next, smoothed.reshape(2, LEV, columns)


def solution(mesh):
    placed = (
        P(None, None, "cols"),
        P(None, None, None, "cols"),
        P("cols"),
        P("cols"),
        P("cols", None),
    )
    return jax.shard_map(
        functools.partial(on_device, mesh.shape["cols"]),
        mesh=mesh,
        in_specs=placed,
        out_specs=(P(None, None, None, "cols"), P(None, None, "cols")),
        check_vma=False,
    )
```

```python
import functools

import numpy as np
import jax
import jax.numpy as jnp
from jax import lax
from jax.experimental import pallas as pl
from jax.experimental.pallas import tpu as pltpu
from jax.sharding import PartitionSpec as P

LEV = 72
CRM_NX = 32
CRM_LEV = 58
PCOL = 4
NBR = 8
WIDTH = 128
SIDE = 64
VMEM_BYTES = 40 * 1024 * 1024
CHUNK = 256

RELAX = 0.5
STEP = 0.5
MIXING = 0.2
LATENT = 0.6
SMOOTHING = 0.5

MESH = pl.DeviceIdType.MESH
F32 = jnp.float32
BF16 = jnp.bfloat16


def interpolation(rows_out, rows_in):
    target = np.arange(rows_out, dtype=np.int32)[:, None]
    source = np.arange(rows_in, dtype=np.int32)[None, :]
    scaled = target * (rows_in - 1)
    lower = scaled // (rows_out - 1)
    weight = (scaled - lower * (rows_out - 1)).astype(np.float32) / np.float32(rows_out - 1)
    upper = np.minimum(lower + 1, rows_in - 1)
    zero = np.float32(0.0)
    return np.where(source == lower, np.float32(1.0) - weight, zero) + np.where(
        source == upper, weight, zero
    )


def interpolation_padded(rows_out, rows_in, height, width):
    matrix = np.zeros((height, width), np.float32)
    matrix[:rows_out, :rows_in] = interpolation(rows_out, rows_in)
    return matrix


def halves(values):
    high = values.astype(BF16)
    low = (values - high.astype(F32)).astype(BF16)
    return high, low


def dot(a, b, dims):
    return lax.dot_general(a, b, (dims, ((), ())), preferred_element_type=F32)


AB = ((1,), (0,))
ABT = ((1,), (1,))


def split_dot(values, chosen, dims):
    rows = values.shape[0]
    both = dot(jnp.concatenate(halves(values), axis=0), chosen, dims)
    return both[:rows] + both[rows:]


def exact_dot(a, b):
    return lax.dot_general(
        a,
        b,
        (AB, ((), ())),
        precision=lax.Precision.HIGHEST,
        preferred_element_type=F32,
    )


def onehot(mask):
    return jnp.where(mask, 1.0, 0.0).astype(BF16)


def pack(pick, values, buffer):
    devices, rows, _ = buffer.shape
    half = devices * rows
    parts = jnp.concatenate(halves(values), axis=0)
    step = min(CHUNK, half)
    lanes = lax.broadcasted_iota(jnp.int32, (step, WIDTH), 1)
    for at in range(0, half, step):
        first = dot(pick[at : at + step, :], parts, ABT)
        second = dot(pick[half + at : half + at + step, :], parts, ABT)
        first = first + pltpu.roll(first, SIDE, 1)
        second = second + pltpu.roll(second, SIDE, 1)
        folded = jnp.where(lanes < SIDE, first, second)
        buffer[at // rows : (at + step) // rows] = folded.reshape(step // rows, rows, WIDTH)


def unpack(buffer, pick):
    devices, rows, _ = buffer.shape
    turned = buffer[...].reshape(devices * rows, WIDTH).T
    return split_dot(jnp.concatenate([turned[:SIDE], turned[SIDE:]], axis=1), pick[...], AB)


def kernel(
    devices,
    gcm_hbm,
    crm_hbm,
    span_hbm,
    cost_hbm,
    near_hbm,
    down_hbm,
    up_hbm,
    next_ref,
    smooth_ref,
    gcm_ref,
    span_ref,
    cost_ref,
    near_ref,
    down_ref,
    up_ref,
    crm_buf,
    fields,
    condensed,
    pick_out,
    pick_in,
    sent,
    arrived,
    sent_back,
    arrived_back,
    start_mean,
    forcing,
    change,
    own_mean,
    near_mean,
    near_pick,
    load_sem,
    out_send,
    out_recv,
    back_send,
    back_recv,
    near_send,
    near_recv,
):
    me = lax.axis_index("cols")
    columns = gcm_ref.shape[2]
    elements = near_ref.shape[1]
    capacity = 2 * columns // devices
    rows = sent.shape[2]
    half = devices * rows
    column_bits = columns.bit_length() - 1

    barrier = pltpu.get_barrier_semaphore()

    def greet(k, carry):
        pl.semaphore_signal(
            barrier, inc=1, device_id=(lax.rem(me + k, devices),), device_id_type=MESH
        )
        return carry

    lax.fori_loop(1, devices, greet, 0)

    loads = [
        pltpu.make_async_copy(source, landing, load_sem.at[i])
        for i, (source, landing) in enumerate(
            (
                (span_hbm, span_ref),
                (gcm_hbm, gcm_ref),
                (down_hbm, down_ref),
                (cost_hbm, cost_ref),
                (crm_hbm, crm_buf.at[:, pl.ds(1, CRM_LEV)]),
                (near_hbm, near_ref),
                (up_hbm, up_ref),
            )
        )
    ]
    for load in loads:
        load.start()
    loads[0].wait()

    span = span_ref[...]
    target = lax.shift_right_logical(span, column_bits)
    place = jnp.bitwise_and(span, columns - 1)
    peers = lax.broadcasted_iota(jnp.int32, (devices, columns), 0)
    mine = peers == target
    first = lax.broadcasted_iota(jnp.int32, (columns, columns), 0)
    second = lax.broadcasted_iota(jnp.int32, (columns, columns), 1)
    before = dot(onehot(mine), onehot(first < second), AB)
    slot = before + (peers * rows).astype(F32)
    if capacity > rows:
        slot = jnp.where(before < rows, slot, slot + (half - rows))
    position = jnp.sum(jnp.where(mine, slot, 0.0), axis=0, keepdims=True).astype(jnp.int32)
    for at in range(0, 2 * half, CHUNK):
        index = lax.broadcasted_iota(jnp.int32, (CHUNK, columns), 0) + at
        pick_out[at : at + CHUNK, :] = onehot(index == position)

    row = lax.broadcasted_iota(jnp.int32, (SIDE, columns), 0)
    for load in loads[1:4]:
        load.wait()
    message = exact_dot(down_ref[...], gcm_ref[1])
    message = jnp.where(row == CRM_LEV, (place + 1).astype(F32), message)
    message = jnp.where(row == CRM_LEV + 1, cost_ref[...].astype(F32), message)
    pack(pick_out, message, sent.at[1])

    pl.semaphore_wait(barrier, devices - 1)

    def relay(source, landing, send_sem, recv_sem):
        def send(k, carry):
            peer = lax.rem(me + devices // 2 + k - 1 + (2 * k - 1) // devices, devices)
            pltpu.make_async_remote_copy(
                src_ref=source.at[peer],
                dst_ref=landing.at[me],
                send_sem=send_sem,
                recv_sem=recv_sem,
                device_id=(peer,),
                device_id_type=MESH,
            ).start()
            return carry

        lax.fori_loop(1, devices, send, 0)
        landing[me] = source[me]
        return pltpu.make_async_remote_copy(
            src_ref=source.at[pl.ds(0, devices - 1)],
            dst_ref=landing.at[pl.ds(0, devices - 1)],
            send_sem=send_sem,
            recv_sem=recv_sem,
            device_id=(lax.rem(me + 1, devices),),
            device_id_type=MESH,
        )

    outward = [None, relay(sent.at[1], arrived.at[1], out_send.at[1], out_recv.at[1])]
    pack(pick_out, exact_dot(down_ref[...], gcm_ref[0]), sent.at[0])
    outward[0] = relay(sent.at[0], arrived.at[0], out_send.at[0], out_recv.at[0])

    for load in loads[4:]:
        load.wait()
    for field in range(2):
        crm_buf[field, 0] = crm_buf[field, 1]
        crm_buf[field, CRM_LEV + 1] = crm_buf[field, CRM_LEV]

    def stencil(here, above, below):
        sideways = pltpu.roll(here, 1, 0) + pltpu.roll(here, CRM_NX - 1, 0)
        return here + (STEP * MIXING) * ((sideways + (above + below)) - 4.0 * here)

    for field in (1, 0):

        def prepare(j, carry, field=field):
            here = crm_buf[field, j + 1].astype(F32)
            above = crm_buf[field, j + 2].astype(F32)
            below = crm_buf[field, j].astype(F32)
            fields[field, j + 1] = stencil(here, above, below)
            start_mean[field, pl.ds(j, 1), :] = jnp.sum(here, axis=0, keepdims=True) * (
                1.0 / CRM_NX
            )
            return carry

        start_mean[field, CRM_LEV:, :] = jnp.zeros((SIDE - CRM_LEV, columns), F32)
        change[field, CRM_LEV:, :] = jnp.zeros((SIDE - CRM_LEV, columns), F32)
        lax.fori_loop(0, CRM_LEV, prepare, 0)

    near = near_ref[...]
    total = devices * elements
    offset = near - (me - 1) * elements
    offset = jnp.where(offset < 0, offset + total, offset)
    offset = jnp.where(offset >= total, offset - total, offset)
    offset = jnp.where(near >= 0, offset, -1)
    spots = lax.broadcasted_iota(jnp.int32, (3 * elements, elements), 0)
    chosen = jnp.zeros((3 * elements, elements), F32)
    for s in range(NBR):
        chosen = chosen + jnp.where(offset[s : s + 1, :] == spots, 1.0, 0.0)
    near_pick[...] = chosen.astype(BF16)
    count = jnp.sum(chosen, axis=0, keepdims=True)
    scale = 1.0 / count

    outward[1].wait_recv()
    landed = arrived[1].reshape(half, WIDTH)
    columns_at = lax.broadcasted_iota(jnp.int32, (half, columns), 1) + 1
    for side in range(2):
        lane = side * SIDE + CRM_LEV
        labels = landed[:, lane : lane + 1].astype(jnp.int32)
        pick_in[side * half : (side + 1) * half, :] = onehot(labels == columns_at)

    def force(field):
        placed = unpack(arrived.at[field], pick_in)
        forcing[field] = (STEP * RELAX) * (placed - start_mean[field])
        return placed

    def close(field):
        fields[field, 0] = fields[field, 1]
        fields[field, CRM_LEV + 1] = fields[field, CRM_LEV]

    def finish(field, j, final):
        next_ref[field, j] = final.astype(BF16)
        at = pl.ds(j, 1)
        change[field, at, :] = (
            jnp.sum(final, axis=0, keepdims=True) * (1.0 / CRM_NX) - start_mean[field, at, :]
        )

    def send_back(field):
        pack(pick_in, change[field], sent_back.at[field])
        return relay(
            sent_back.at[field], arrived_back.at[field], back_send.at[field], back_recv.at[field]
        )

    top = force(1)[CRM_LEV + 1 : CRM_LEV + 2, :]

    def condense(j, step, moisture):
        level = j.astype(F32)
        saturation = 1.0 - 0.8 * level / (CRM_LEV - 1)
        active = jnp.where(level < top, 1.0, 0.0)
        taken = jnp.maximum(moisture - saturation, 0.0) * active
        condensed[step, j] = taken
        return moisture - taken

    def first_moisture(j, carry):
        moisture = fields[1, j + 1] + forcing[1, pl.ds(j, 1), :]
        fields[1, j + 1] = condense(j, 0, moisture)
        return carry

    lax.fori_loop(0, CRM_LEV, first_moisture, 0)
    close(1)

    def second_moisture(j, carry):
        moisture = stencil(fields[1, j + 1], fields[1, j + 2], fields[1, j])
        finish(1, j, condense(j, 1, moisture + forcing[1, pl.ds(j, 1), :]))
        return carry

    lax.fori_loop(0, CRM_LEV, second_moisture, 0)
    inward = [None, send_back(1)]

    outward[0].wait_recv()
    force(0)

    def first_heat(j, carry):
        fields[0, j + 1] = fields[0, j + 1] + forcing[0, pl.ds(j, 1), :] + LATENT * condensed[0, j]
        return carry

    lax.fori_loop(0, CRM_LEV, first_heat, 0)
    close(0)

    def second_heat(j, carry):
        heat = stencil(fields[0, j + 1], fields[0, j + 2], fields[0, j])
        finish(0, j, heat + forcing[0, pl.ds(j, 1), :] + LATENT * condensed[1, j])
        return carry

    lax.fori_loop(0, CRM_LEV, second_heat, 0)
    inward[0] = send_back(0)

    member = lax.broadcasted_iota(jnp.int32, (elements, columns), 1)
    lowest = lax.broadcasted_iota(jnp.int32, (elements, columns), 0) * PCOL
    inside = onehot((member >= lowest) & (member < lowest + PCOL))
    exchanges = [[], []]
    for field in (1, 0):
        inward[field].wait_recv()
        updated = gcm_ref[field] + exact_dot(up_ref[...], unpack(arrived_back.at[field], pick_out))
        smooth_ref[field] = updated
        own_mean[field] = split_dot(updated, inside, ABT) * (1.0 / PCOL)
        for side in range(2):
            peer = lax.rem(me + 1, devices) if side == 0 else lax.rem(me + devices - 1, devices)
            exchange = pltpu.make_async_remote_copy(
                src_ref=own_mean.at[field],
                dst_ref=near_mean.at[field, side],
                send_sem=near_send.at[field, side],
                recv_sem=near_recv.at[field, side],
                device_id=(peer,),
                device_id_type=MESH,
            )
            exchange.start()
            exchanges[field].append(exchange)
    for field in (1, 0):
        edge_mean = own_mean[field]
        around = split_dot(edge_mean, near_pick[elements : 2 * elements, :], AB)
        for side in range(2):
            exchanges[field][side].wait_recv()
            spot = 2 * side * elements
            around = around + split_dot(
                near_mean[field, side], near_pick[spot : spot + elements, :], AB
            )
        pull = SMOOTHING * (around * scale - edge_mean)
        smooth_ref[field] = smooth_ref[field] + split_dot(pull, inside, AB)

    for field in (1, 0):
        outward[field].wait_send()
        inward[field].wait_send()
        for exchange in exchanges[field]:
            exchange.wait_send()


def on_device(devices, gcm_state, crm_state, span_map, crm_cost, neighbours):
    columns = gcm_state.shape[2]
    elements = neighbours.shape[0]
    rows = max(8, columns // devices)
    slots = 2 * devices * rows
    down = jnp.asarray(interpolation_padded(CRM_LEV, LEV, SIDE, LEV))
    up = jnp.asarray(interpolation_padded(LEV, CRM_LEV, LEV, SIDE))
    vmem = pl.BlockSpec(memory_space=pltpu.VMEM)
    hbm = pl.BlockSpec(memory_space=pltpu.HBM)
    relay = pltpu.VMEM((2, devices, rows, WIDTH), F32)
    per_level = pltpu.VMEM((2, SIDE, columns), F32)
    pair = pltpu.SemaphoreType.DMA((2,))
    crm_next, smoothed = pl.pallas_call(
        functools.partial(kernel, devices),
        out_shape=(
            jax.ShapeDtypeStruct(crm_state.shape, BF16),
            jax.ShapeDtypeStruct((2, LEV, columns), F32),
        ),
        in_specs=[hbm] * 7,
        out_specs=(vmem, vmem),
        scratch_shapes=[
            pltpu.VMEM((2, LEV, columns), F32),
            pltpu.VMEM((1, columns), jnp.int32),
            pltpu.VMEM((1, columns), jnp.int32),
            pltpu.VMEM((NBR, elements), jnp.int32),
            pltpu.VMEM((SIDE, LEV), F32),
            pltpu.VMEM((LEV, SIDE), F32),
            pltpu.VMEM((2, CRM_LEV + 2, CRM_NX, columns), BF16),
            pltpu.VMEM((2, CRM_LEV + 2, CRM_NX, columns), F32),
            pltpu.VMEM((2, CRM_LEV, CRM_NX, columns), F32),
            pltpu.VMEM((slots, columns), BF16),
            pltpu.VMEM((slots, columns), BF16),
            relay,
            relay,
            relay,
            relay,
            per_level,
            per_level,
            per_level,
            pltpu.VMEM((2, LEV, elements), F32),
            pltpu.VMEM((2, 2, LEV, elements), F32),
            pltpu.VMEM((3 * elements, elements), BF16),
            pltpu.SemaphoreType.DMA((7,)),
            pair,
            pair,
            pair,
            pair,
            pltpu.SemaphoreType.DMA((2, 2)),
            pltpu.SemaphoreType.DMA((2, 2)),
        ],
        compiler_params=pltpu.CompilerParams(
            collective_id=0, has_side_effects=True, vmem_limit_bytes=VMEM_BYTES
        ),
    )(
        *(
            pltpu.with_memory_space_constraint(x, pltpu.HBM)
            for x in (
                gcm_state,
                crm_state,
                span_map.reshape(1, columns),
                crm_cost.reshape(1, columns),
                neighbours.T,
                down,
                up,
            )
        )
    )
    return crm_next, smoothed


def solution(mesh):
    placed = (
        P(None, None, "cols"),
        P(None, None, None, "cols"),
        P("cols"),
        P("cols"),
        P("cols", None),
    )
    return jax.shard_map(
        functools.partial(on_device, mesh.shape["cols"]),
        mesh=mesh,
        in_specs=placed,
        out_specs=(P(None, None, None, "cols"), P(None, None, "cols")),
        check_vma=False,
    )
```

```python
import functools

import numpy as np
import jax
import jax.numpy as jnp
from jax import lax
from jax.experimental import pallas as pl
from jax.experimental.pallas import tpu as pltpu
from jax.sharding import PartitionSpec as P

LEV = 72
CRM_NX = 32
CRM_LEV = 58
PCOL = 4
NBR = 8
WIDTH = 128
SIDE = 64
VMEM_BYTES = 40 * 1024 * 1024
CHUNK = 256

RELAX = 0.5
STEP = 0.5
MIXING = 0.2
LATENT = 0.6
SMOOTHING = 0.5

MESH = pl.DeviceIdType.MESH
F32 = jnp.float32
BF16 = jnp.bfloat16


def interpolation(rows_out, rows_in):
    target = np.arange(rows_out, dtype=np.int32)[:, None]
    source = np.arange(rows_in, dtype=np.int32)[None, :]
    scaled = target * (rows_in - 1)
    lower = scaled // (rows_out - 1)
    weight = (scaled - lower * (rows_out - 1)).astype(np.float32) / np.float32(rows_out - 1)
    upper = np.minimum(lower + 1, rows_in - 1)
    zero = np.float32(0.0)
    return np.where(source == lower, np.float32(1.0) - weight, zero) + np.where(
        source == upper, weight, zero
    )


def interpolation_padded(rows_out, rows_in, height, width):
    matrix = np.zeros((height, width), np.float32)
    matrix[:rows_out, :rows_in] = interpolation(rows_out, rows_in)
    return matrix


def halves(values):
    high = values.astype(BF16)
    low = (values - high.astype(F32)).astype(BF16)
    return high, low


def dot(a, b, dims):
    return lax.dot_general(a, b, (dims, ((), ())), preferred_element_type=F32)


AB = ((1,), (0,))
ABT = ((1,), (1,))


def split_dot(values, chosen, dims):
    rows = values.shape[0]
    both = dot(jnp.concatenate(halves(values), axis=0), chosen, dims)
    return both[:rows] + both[rows:]


def exact_dot(a, b):
    return lax.dot_general(
        a,
        b,
        (AB, ((), ())),
        precision=lax.Precision.HIGHEST,
        preferred_element_type=F32,
    )


def onehot(mask):
    return jnp.where(mask, 1.0, 0.0).astype(BF16)


def pack(pick, values, buffer):
    devices, rows, _ = buffer.shape
    half = devices * rows
    parts = jnp.concatenate(halves(values), axis=0)
    step = min(CHUNK, half)
    lanes = lax.broadcasted_iota(jnp.int32, (step, WIDTH), 1)
    for at in range(0, half, step):
        first = dot(pick[at : at + step, :], parts, ABT)
        second = dot(pick[half + at : half + at + step, :], parts, ABT)
        first = first + pltpu.roll(first, SIDE, 1)
        second = second + pltpu.roll(second, SIDE, 1)
        folded = jnp.where(lanes < SIDE, first, second)
        buffer[at // rows : (at + step) // rows] = folded.reshape(step // rows, rows, WIDTH)


def unpack(buffer, pick):
    devices, rows, _ = buffer.shape
    turned = buffer[...].reshape(devices * rows, WIDTH).T
    return split_dot(jnp.concatenate([turned[:SIDE], turned[SIDE:]], axis=1), pick[...], AB)


def kernel(
    devices,
    gcm_hbm,
    crm_hbm,
    span_hbm,
    cost_hbm,
    near_hbm,
    down_hbm,
    up_hbm,
    next_ref,
    smooth_ref,
    gcm_ref,
    span_ref,
    cost_ref,
    near_ref,
    down_ref,
    up_ref,
    crm_buf,
    fields,
    condensed,
    pick_out,
    pick_in,
    sent,
    arrived,
    sent_back,
    arrived_back,
    start_mean,
    forcing,
    change,
    own_mean,
    near_mean,
    near_pick,
    load_sem,
    out_send,
    out_recv,
    back_send,
    back_recv,
    near_send,
    near_recv,
):
    me = lax.axis_index("cols")
    columns = gcm_ref.shape[2]
    elements = near_ref.shape[1]
    capacity = 2 * columns // devices
    rows = sent.shape[2]
    half = devices * rows
    column_bits = columns.bit_length() - 1

    barrier = pltpu.get_barrier_semaphore()

    def greet(k, carry):
        pl.semaphore_signal(
            barrier, inc=1, device_id=(lax.rem(me + k, devices),), device_id_type=MESH
        )
        return carry

    lax.fori_loop(1, devices, greet, 0)

    loads = [
        pltpu.make_async_copy(source, landing, load_sem.at[i])
        for i, (source, landing) in enumerate(
            (
                (span_hbm, span_ref),
                (gcm_hbm, gcm_ref),
                (down_hbm, down_ref),
                (cost_hbm, cost_ref),
                (crm_hbm, crm_buf.at[:, pl.ds(1, CRM_LEV)]),
                (near_hbm, near_ref),
                (up_hbm, up_ref),
            )
        )
    ]
    for load in loads:
        load.start()
    loads[0].wait()

    span = span_ref[...]
    target = lax.shift_right_logical(span, column_bits)
    place = jnp.bitwise_and(span, columns - 1)
    peers = lax.broadcasted_iota(jnp.int32, (devices, columns), 0)
    mine = peers == target
    first = lax.broadcasted_iota(jnp.int32, (columns, columns), 0)
    second = lax.broadcasted_iota(jnp.int32, (columns, columns), 1)
    before = dot(onehot(mine), onehot(first < second), AB)
    slot = before + (peers * rows).astype(F32)
    if capacity > rows:
        slot = jnp.where(before < rows, slot, slot + (half - rows))
    position = jnp.sum(jnp.where(mine, slot, 0.0), axis=0, keepdims=True).astype(jnp.int32)
    for at in range(0, 2 * half, CHUNK):
        index = lax.broadcasted_iota(jnp.int32, (CHUNK, columns), 0) + at
        pick_out[at : at + CHUNK, :] = onehot(index == position)

    row = lax.broadcasted_iota(jnp.int32, (SIDE, columns), 0)
    for load in loads[1:4]:
        load.wait()
    message = exact_dot(down_ref[...], gcm_ref[1])
    message = jnp.where(row == CRM_LEV, (place + 1).astype(F32), message)
    message = jnp.where(row == CRM_LEV + 1, cost_ref[...].astype(F32), message)
    pack(pick_out, message, sent.at[1])

    pl.semaphore_wait(barrier, devices - 1)

    def relay(source, landing, send_sem, recv_sem):
        def send(k, carry):
            peer = lax.rem(me + devices // 2 + k - 1 + (2 * k - 1) // devices, devices)
            pltpu.make_async_remote_copy(
                src_ref=source.at[peer],
                dst_ref=landing.at[me],
                send_sem=send_sem,
                recv_sem=recv_sem,
                device_id=(peer,),
                device_id_type=MESH,
            ).start()
            return carry

        lax.fori_loop(1, devices, send, 0)
        landing[me] = source[me]
        return pltpu.make_async_remote_copy(
            src_ref=source.at[pl.ds(0, devices - 1)],
            dst_ref=landing.at[pl.ds(0, devices - 1)],
            send_sem=send_sem,
            recv_sem=recv_sem,
            device_id=(lax.rem(me + 1, devices),),
            device_id_type=MESH,
        )

    outward = [None, relay(sent.at[1], arrived.at[1], out_send.at[1], out_recv.at[1])]
    pack(pick_out, exact_dot(down_ref[...], gcm_ref[0]), sent.at[0])
    outward[0] = relay(sent.at[0], arrived.at[0], out_send.at[0], out_recv.at[0])

    for load in loads[4:]:
        load.wait()
    for field in range(2):
        crm_buf[field, 0] = crm_buf[field, 1]
        crm_buf[field, CRM_LEV + 1] = crm_buf[field, CRM_LEV]

    def stencil(here, above, below):
        sideways = pltpu.roll(here, 1, 0) + pltpu.roll(here, CRM_NX - 1, 0)
        return here + (STEP * MIXING) * ((sideways + (above + below)) - 4.0 * here)

    for field in (1, 0):

        def prepare(j, carry, field=field):
            here = crm_buf[field, j + 1].astype(F32)
            above = crm_buf[field, j + 2].astype(F32)
            below = crm_buf[field, j].astype(F32)
            fields[field, j + 1] = stencil(here, above, below)
            start_mean[field, pl.ds(j, 1), :] = jnp.sum(here, axis=0, keepdims=True) * (
                1.0 / CRM_NX
            )
            return carry

        start_mean[field, CRM_LEV:, :] = jnp.zeros((SIDE - CRM_LEV, columns), F32)
        change[field, CRM_LEV:, :] = jnp.zeros((SIDE - CRM_LEV, columns), F32)
        lax.fori_loop(0, CRM_LEV, prepare, 0)

    near = near_ref[...]
    total = devices * elements
    offset = near - (me - 1) * elements
    offset = jnp.where(offset < 0, offset + total, offset)
    offset = jnp.where(offset >= total, offset - total, offset)
    offset = jnp.where(near >= 0, offset, -1)
    spots = lax.broadcasted_iota(jnp.int32, (3 * elements, elements), 0)
    chosen = jnp.zeros((3 * elements, elements), F32)
    for s in range(NBR):
        chosen = chosen + jnp.where(offset[s : s + 1, :] == spots, 1.0, 0.0)
    near_pick[...] = chosen.astype(BF16)
    count = jnp.sum(chosen, axis=0, keepdims=True)
    scale = 1.0 / count

    outward[1].wait_recv()
    landed = arrived[1].reshape(half, WIDTH)
    columns_at = lax.broadcasted_iota(jnp.int32, (half, columns), 1) + 1
    for side in range(2):
        lane = side * SIDE + CRM_LEV
        labels = landed[:, lane : lane + 1].astype(jnp.int32)
        pick_in[side * half : (side + 1) * half, :] = onehot(labels == columns_at)

    def force(field):
        placed = unpack(arrived.at[field], pick_in)
        forcing[field] = (STEP * RELAX) * (placed - start_mean[field])
        return placed

    def close(field):
        fields[field, 0] = fields[field, 1]
        fields[field, CRM_LEV + 1] = fields[field, CRM_LEV]

    def finish(field, j, final):
        next_ref[field, j] = final.astype(BF16)
        at = pl.ds(j, 1)
        change[field, at, :] = (
            jnp.sum(final, axis=0, keepdims=True) * (1.0 / CRM_NX) - start_mean[field, at, :]
        )

    def send_back(field):
        pack(pick_in, change[field], sent_back.at[field])
        return relay(
            sent_back.at[field], arrived_back.at[field], back_send.at[field], back_recv.at[field]
        )

    top = force(1)[CRM_LEV + 1 : CRM_LEV + 2, :]

    def condense(j, step, moisture):
        level = j.astype(F32)
        saturation = 1.0 - 0.8 * level / (CRM_LEV - 1)
        active = jnp.where(level < top, 1.0, 0.0)
        taken = jnp.maximum(moisture - saturation, 0.0) * active
        condensed[step, j] = taken
        return moisture - taken

    def first_moisture(j, carry):
        moisture = fields[1, j + 1] + forcing[1, pl.ds(j, 1), :]
        fields[1, j + 1] = condense(j, 0, moisture)
        return carry

    lax.fori_loop(0, CRM_LEV, first_moisture, 0)
    close(1)

    def second_moisture(j, carry):
        moisture = stencil(fields[1, j + 1], fields[1, j + 2], fields[1, j])
        finish(1, j, condense(j, 1, moisture + forcing[1, pl.ds(j, 1), :]))
        return carry

    lax.fori_loop(0, CRM_LEV, second_moisture, 0)
    inward = [None, send_back(1)]

    outward[0].wait_recv()
    force(0)

    def first_heat(j, carry):
        fields[0, j + 1] = fields[0, j + 1] + forcing[0, pl.ds(j, 1), :] + LATENT * condensed[0, j]
        return carry

    lax.fori_loop(0, CRM_LEV, first_heat, 0)
    close(0)

    def second_heat(j, carry):
        heat = stencil(fields[0, j + 1], fields[0, j + 2], fields[0, j])
        finish(0, j, heat + forcing[0, pl.ds(j, 1), :] + LATENT * condensed[1, j])
        return carry

    lax.fori_loop(0, CRM_LEV, second_heat, 0)
    inward[0] = send_back(0)

    member = lax.broadcasted_iota(jnp.int32, (elements, columns), 1)
    lowest = lax.broadcasted_iota(jnp.int32, (elements, columns), 0) * PCOL
    inside = onehot((member >= lowest) & (member < lowest + PCOL))
    exchanges = [[], []]
    for field in (1, 0):
        still_mean = split_dot(gcm_ref[field], inside, ABT)
        inward[field].wait_recv()
        own = unpack(arrived_back.at[field], pick_out)
        moved = exact_dot(up_ref[...], split_dot(own, inside, ABT))
        own_mean[field] = (still_mean + moved) * (1.0 / PCOL)
        for side in range(2):
            peer = lax.rem(me + 1, devices) if side == 0 else lax.rem(me + devices - 1, devices)
            exchange = pltpu.make_async_remote_copy(
                src_ref=own_mean.at[field],
                dst_ref=near_mean.at[field, side],
                send_sem=near_send.at[field, side],
                recv_sem=near_recv.at[field, side],
                device_id=(peer,),
                device_id_type=MESH,
            )
            exchange.start()
            exchanges[field].append(exchange)
        smooth_ref[field] = gcm_ref[field] + exact_dot(up_ref[...], own)
    for field in (1, 0):
        edge_mean = own_mean[field]
        around = split_dot(edge_mean, near_pick[elements : 2 * elements, :], AB)
        for side in range(2):
            exchanges[field][side].wait_recv()
            spot = 2 * side * elements
            around = around + split_dot(
                near_mean[field, side], near_pick[spot : spot + elements, :], AB
            )
        pull = SMOOTHING * (around * scale - edge_mean)
        smooth_ref[field] = smooth_ref[field] + split_dot(pull, inside, AB)

    for field in (1, 0):
        outward[field].wait_send()
        inward[field].wait_send()
        for exchange in exchanges[field]:
            exchange.wait_send()


def on_device(devices, gcm_state, crm_state, span_map, crm_cost, neighbours):
    columns = gcm_state.shape[2]
    elements = neighbours.shape[0]
    rows = max(8, columns // devices)
    slots = 2 * devices * rows
    down = jnp.asarray(interpolation_padded(CRM_LEV, LEV, SIDE, LEV))
    up = jnp.asarray(interpolation_padded(LEV, CRM_LEV, LEV, SIDE))
    vmem = pl.BlockSpec(memory_space=pltpu.VMEM)
    hbm = pl.BlockSpec(memory_space=pltpu.HBM)
    relay = pltpu.VMEM((2, devices, rows, WIDTH), F32)
    per_level = pltpu.VMEM((2, SIDE, columns), F32)
    pair = pltpu.SemaphoreType.DMA((2,))
    crm_next, smoothed = pl.pallas_call(
        functools.partial(kernel, devices),
        out_shape=(
            jax.ShapeDtypeStruct(crm_state.shape, BF16),
            jax.ShapeDtypeStruct((2, LEV, columns), F32),
        ),
        in_specs=[hbm] * 7,
        out_specs=(vmem, vmem),
        scratch_shapes=[
            pltpu.VMEM((2, LEV, columns), F32),
            pltpu.VMEM((1, columns), jnp.int32),
            pltpu.VMEM((1, columns), jnp.int32),
            pltpu.VMEM((NBR, elements), jnp.int32),
            pltpu.VMEM((SIDE, LEV), F32),
            pltpu.VMEM((LEV, SIDE), F32),
            pltpu.VMEM((2, CRM_LEV + 2, CRM_NX, columns), BF16),
            pltpu.VMEM((2, CRM_LEV + 2, CRM_NX, columns), F32),
            pltpu.VMEM((2, CRM_LEV, CRM_NX, columns), F32),
            pltpu.VMEM((slots, columns), BF16),
            pltpu.VMEM((slots, columns), BF16),
            relay,
            relay,
            relay,
            relay,
            per_level,
            per_level,
            per_level,
            pltpu.VMEM((2, LEV, elements), F32),
            pltpu.VMEM((2, 2, LEV, elements), F32),
            pltpu.VMEM((3 * elements, elements), BF16),
            pltpu.SemaphoreType.DMA((7,)),
            pair,
            pair,
            pair,
            pair,
            pltpu.SemaphoreType.DMA((2, 2)),
            pltpu.SemaphoreType.DMA((2, 2)),
        ],
        compiler_params=pltpu.CompilerParams(
            collective_id=0, has_side_effects=True, vmem_limit_bytes=VMEM_BYTES
        ),
    )(
        *(
            pltpu.with_memory_space_constraint(x, pltpu.HBM)
            for x in (
                gcm_state,
                crm_state,
                span_map.reshape(1, columns),
                crm_cost.reshape(1, columns),
                neighbours.T,
                down,
                up,
            )
        )
    )
    return crm_next, smoothed


def solution(mesh):
    placed = (
        P(None, None, "cols"),
        P(None, None, None, "cols"),
        P("cols"),
        P("cols"),
        P("cols", None),
    )
    return jax.shard_map(
        functools.partial(on_device, mesh.shape["cols"]),
        mesh=mesh,
        in_specs=placed,
        out_specs=(P(None, None, None, "cols"), P(None, None, "cols")),
        check_vma=False,
    )
```
